256 devices in a mesh: head: 8 (over x, z_lo), ctx: 32 (over y, z_hi, core).
Axes of the slice: x: 4, y: 4, z: 8 (z_hi: 4, z_lo: 2; z = z_hi * 2 + z_lo), core: 2. Of those that a mesh axis runs over, the one named last changes fastest.
Arguments:
- queries: bfloat16 [16384, 5120], P(('head', 'ctx')), may hold values from -6 to 6
- keys: bfloat16 [16384, 5120], P(('head', 'ctx')), may hold values from -6 to 6
- values: bfloat16 [16384, 5120], P(('head', 'ctx')), may hold values from -6 to 6
- rates: bfloat16 [16384, 8], P(('head', 'ctx')), may hold values from 0.099609375 to 1
- q_gain: float32 [5120], replicated, may hold values from 0.1 to 1.9
- k_gain: float32 [5120], replicated, may hold values from 0.2 to 4.5, as said below
- w_first: float32 [8, 640, 640], P('head'), may hold values from -0.2766993 to 0.2766993
- w_second: float32 [8, 640, 640], P('head'), may hold values from -0.25 to 0.25
- w_third: float32 [8, 640, 640], P('head'), may hold values from -0.2766993 to 0.2766993
Outputs:
- attended: bfloat16 [16384, 5120], P(('head', 'ctx'))
The draws below stay inside these ranges and needn't reach their ends.
Inputs may be any that keep to these rules, and one draw needn't show every extreme that they name: `k_gain`: positive per-feature gains.
All inputs are finite; a program needn't handle non-finite values.
Results may differ from the reference program's by a relative error of at most 0.015.
Values may be sent and summed in bfloat16 or wider, within the bound.
A program may use at most 64 MiB of HBM per device.

```python
import math
import jax
import jax.numpy as jnp
from jax import lax

HEADS = 8
HD = 640
NS_STEPS = 2
D = 5120
SPAN = 16384


def draw_k_gain(key, part):
    fraction = (jnp.arange(D) % HD).astype(jnp.float32) / HD
    jitter = jax.random.uniform(key, (D,), jnp.float32, 0.8, 1.25)
    return jnp.power(10.0, fraction - 0.5) * jitter


def fast_weight(key):
    fraction = jnp.arange(HD).astype(jnp.float32) / HD
    entries = jnp.clip(jax.random.normal(key, (HEADS, HD, HD), jnp.float32), -3.0, 3.0)
    column = jnp.power(10.0, 0.5 * fraction - 0.25)
    jitter = jax.random.uniform(jax.random.fold_in(key, 7), (HEADS, 1, HD), jnp.float32, 0.8, 1.25)
    return entries * column * jitter / jnp.sqrt(jnp.float32(HD))


def draw_w_first(key, part):
    return fast_weight(jax.random.fold_in(key, 11))


def draw_w_third(key, part):
    return fast_weight(jax.random.fold_in(key, 13))


def steps_of(rng, extent, split, smallest, largest):
    factor_of, own = 1.0, jax.random.fold_in(rng, 6)
    for dim, shards_of in split:
        heights = jnp.exp(jax.random.uniform(jax.random.fold_in(own, dim), (shards_of,), jnp.float32, smallest / len(split), largest / len(split)))
        factor_of = factor_of * jnp.repeat(heights, extent[dim] // shards_of).reshape([-1 if axis == dim else 1 for axis in range(len(extent))])
    return factor_of


def gaussian(key, dims, deviation, reach, split=(), held_as=jnp.bfloat16):
    array = deviation * jax.random.normal(key, dims, jnp.float32)
    if split:
        array = array * steps_of(key, dims, split, -0.22, 0.18)
    return jnp.clip(array, -reach, reach).astype(held_as)


def setup_inputs(seed: int = 0) -> dict:
    key_of = jax.random.split(jax.random.key(seed), 10)
    return {
        "queries": gaussian(key_of[0], (SPAN, D), 1.0, 6.0, ((0, 256),)),
        "keys": gaussian(key_of[1], (SPAN, D), 1.0, 6.0, ((0, 256),)),
        "values": gaussian(key_of[2], (SPAN, D), 1.0, 6.0, ((0, 256),)),
        "rates": jnp.clip(jnp.exp(math.log(1.0) - 2.306499 * jax.random.uniform(key_of[3], (SPAN, HEADS), jnp.float32) ** steps_of(key_of[3], (SPAN, HEADS), ((0, 256),), -0.2, 0.2)), 0.099609375, 1.0).astype(jnp.bfloat16),
        "q_gain": jnp.clip(1.0 + 0.18 * jax.random.normal(key_of[4], (D,), jnp.float32), 0.1, 1.9),
        "k_gain": draw_k_gain(jax.random.fold_in(key_of[9], 71), 0),
        "w_first": draw_w_first(jax.random.fold_in(key_of[9], 71), 0),
        "w_second": gaussian(key_of[7], (HEADS, HD, HD), HD ** -0.5, 0.25, ((0, 8),), jnp.float32),
        "w_third": draw_w_third(jax.random.fold_in(key_of[9], 71), 0),
    }


epsilon = 1e-06
frob_eps = 1e-07
coeff_a = 3.4445
coeff_b = -4.775
coeff_c = 2.0315
step_size = 1.0

def rms_scale(inputs, gain):
    widened = inputs.astype(jnp.float32)
    factor = lax.rsqrt(lax.optimization_barrier(jnp.mean(widened * widened, axis=-1, keepdims=True)) + epsilon)
    return (widened * factor * gain.astype(jnp.float32)).astype(jnp.bfloat16)

def newton_schulz(gradient):
    frob_total = jnp.sqrt(jnp.sum(gradient * gradient))
    iterate = (gradient / (frob_total + frob_eps)).astype(jnp.bfloat16)
    for repeat_index in range(NS_STEPS):
        square = jnp.dot(iterate, iterate.T, preferred_element_type=jnp.float32).astype(jnp.bfloat16)
        polynomial = (coeff_b * square.astype(jnp.float32) + coeff_c * jnp.dot(square, square, preferred_element_type=jnp.float32)).astype(jnp.bfloat16)
        iterate = (coeff_a * iterate.astype(jnp.float32) + jnp.dot(polynomial, iterate, preferred_element_type=jnp.float32)).astype(jnp.bfloat16)
    return iterate

def reference(queries, keys, values, rates, q_gain, k_gain, w_first, w_second, w_third):
    queries_n = rms_scale(queries, q_gain)
    keys_n = rms_scale(keys, k_gain)

    def one_head(head_index):
        start = (head_index * HD).astype(jnp.int32)
        query_block = lax.dynamic_slice_in_dim(queries_n, start, HD, 1)
        key_block = lax.dynamic_slice_in_dim(keys_n, start, HD, 1)
        value_block = lax.dynamic_slice_in_dim(values, start, HD, 1)
        rate_block = lax.dynamic_slice_in_dim(rates, head_index.astype(jnp.int32), 1, 1)
        first = w_first[head_index]
        second = w_second[head_index]
        third = w_third[head_index]
        first_b = first.astype(jnp.bfloat16)
        second_b = second.astype(jnp.bfloat16)
        third_b = third.astype(jnp.bfloat16)
        pre_first = jnp.dot(key_block, first_b, preferred_element_type=jnp.float32)
        pre_third = jnp.dot(key_block, third_b, preferred_element_type=jnp.float32)
        sigmoid = jax.nn.sigmoid(pre_first)
        activ = pre_first * sigmoid
        hidden = (activ * pre_third).astype(jnp.bfloat16)
        scaled_v = (rate_block.astype(jnp.float32) * value_block.astype(jnp.float32)).astype(jnp.bfloat16)
        back_hidden = jnp.dot(scaled_v, second_b.T, preferred_element_type=jnp.float32)
        grad_pre_first = (back_hidden * pre_third * sigmoid * (1.0 + pre_first * (1.0 - sigmoid))).astype(jnp.bfloat16)
        grad_pre_third = (back_hidden * activ).astype(jnp.bfloat16)
        grad_first = jnp.dot(key_block.T, grad_pre_first, preferred_element_type=jnp.float32)
        grad_second = jnp.dot(hidden.T, scaled_v, preferred_element_type=jnp.float32)
        grad_third = jnp.dot(key_block.T, grad_pre_third, preferred_element_type=jnp.float32)
        new_first = (first + step_size * newton_schulz(grad_first).astype(jnp.float32)).astype(jnp.bfloat16)
        new_second = (second + step_size * newton_schulz(grad_second).astype(jnp.float32)).astype(jnp.bfloat16)
        new_third = (third + step_size * newton_schulz(grad_third).astype(jnp.float32)).astype(jnp.bfloat16)
        query_first = jnp.dot(query_block, new_first, preferred_element_type=jnp.float32)
        query_third = jnp.dot(query_block, new_third, preferred_element_type=jnp.float32)
        gated = (jax.nn.silu(query_first) * query_third).astype(jnp.bfloat16)
        result = jnp.dot(gated, new_second, preferred_element_type=jnp.float32)
        factor = lax.rsqrt(lax.optimization_barrier(jnp.mean(result * result, axis=-1, keepdims=True)) + epsilon)
        return (result * factor).astype(jnp.bfloat16)
    blocks = lax.map(one_head, jnp.arange(HEADS, dtype=jnp.int32))
    return jnp.transpose(blocks, (1, 0, 2)).reshape(SPAN, HEADS * HD)
```

```python
import functools

import jax
import jax.numpy as jnp
from jax import lax
from jax.experimental import pallas as pl
from jax.experimental.pallas import tpu as pltpu
from jax.sharding import PartitionSpec as P

MESH = pl.DeviceIdType.MESH
F32 = jnp.float32
BF16 = jnp.bfloat16

epsilon = 1e-06
frob_eps = 1e-07
coeff_a = 3.4445
coeff_b = -4.775
coeff_c = 2.0315
step_size = 1.0

NY, NZ = 4, 4
PIECE = 24


def dot(a, b):
    return jnp.dot(a, b, preferred_element_type=F32)


def dot_t(a, b):
    return lax.dot_general(a, b, (((1,), (1,)), ((), ())), preferred_element_type=F32)


def kernel(
    nh,
    q_ref, k_ref, v_ref, r_ref, qg_ref, kg_ref, w1_hbm, w2_hbm, w3_hbm,
    out_ref,
    sent, got, wf, wb, t1, t3, hid, d1, d3, kt, ht,
    own, cs, cr, ys, yr, zq, zs, zr, zg, x0, xs, xm, x1, u, fw, ob, orx,
    w_sem, a_ss, a_rs, c_ss, c_rs, y_ss, y_rs, z_ss, z_rs, zg_ss, zg_rs,
    yg_ss, yg_rs, cg_ss, cg_rs, o_ss, o_rs,
):
    me_h = lax.axis_index("head")
    me_c = lax.axis_index("ctx")
    y = me_c // (2 * NZ)
    z = (me_c // 2) % NZ
    core = me_c % 2
    tok, width = sent.shape[2], sent.shape[3]
    half = width // 2
    block = half // NY

    def head_peer(s):
        return (me_h + s) % nh

    def ctx_of(yy, zz, cc):
        return (yy * NZ + zz) * 2 + cc

    def y_dev(yy):
        return (me_h, ctx_of(yy, z, core))

    def z_dev(zz):
        return (me_h, ctx_of(y, zz, core))

    core_dev = (me_h, ctx_of(y, z, 1 - core))

    def remote(src, dst, ss, rs, dev):
        return pltpu.make_async_remote_copy(
            src_ref=src, dst_ref=dst, send_sem=ss, recv_sem=rs, device_id=dev, device_id_type=MESH
        )

    w_copies = [
        pltpu.make_async_copy(w.at[0], wf.at[i], w_sem.at[i])
        for i, w in enumerate((w1_hbm, w2_hbm, w3_hbm))
    ]
    for copy in w_copies:
        copy.start()

    barrier = pltpu.get_barrier_semaphore()

    def greet(dev):
        pl.semaphore_signal(barrier, inc=1, device_id=dev, device_id_type=MESH)

    for s in range(1, nh):
        greet((head_peer(s), me_c))
    for s in range(1, NY):
        greet(y_dev((y + s) % NY))
    for s in range(1, NZ):
        greet(z_dev((z + s) % NZ))
    greet(core_dev)

    def normalize(x_ref, g_ref, t):
        total = jnp.zeros((tok, 1), F32)
        for j in range(nh):
            x = x_ref[:, j * width : (j + 1) * width].astype(F32)
            total = total + jnp.sum(x * x, axis=-1, keepdims=True)
        factor = lax.rsqrt(total / (nh * width) + epsilon)
        for j in range(nh):
            cols = slice(j * width, (j + 1) * width)
            sent[t, j] = (x_ref[:, cols].astype(F32) * factor * g_ref[:, cols]).astype(BF16)

    def exchange(t):
        def step(s, carry):
            j = head_peer(s)
            remote(
                sent.at[t, j], got.at[t, me_h], a_ss.at[t, j], a_rs.at[t, me_h], (j, me_c)
            ).start()
            return carry

        lax.fori_loop(1, nh, step, 0)
        got[t, me_h] = sent[t, me_h]

    def arrived(t):
        def step(s, carry):
            j = head_peer(s)
            remote(
                sent.at[t, j], got.at[t, j], a_ss.at[t, j], a_rs.at[t, j], (j, me_c)
            ).wait()
            return carry

        lax.fori_loop(1, nh, step, 0)

    normalize(k_ref, kg_ref, 0)
    pl.semaphore_wait(barrier, nh - 1 + NY - 1 + NZ - 1 + 1)
    exchange(0)
    rate = r_ref[...].astype(F32)
    for j in range(nh):
        cols = slice(j * width, (j + 1) * width)
        sent[1, j] = (rate[:, j : j + 1] * v_ref[:, cols].astype(F32)).astype(BF16)
    exchange(1)
    normalize(q_ref, qg_ref, 2)
    exchange(2)

    for i in range(3):
        w_copies[i].wait()
        wb[i] = wf[i].astype(BF16)

    tokens = nh * tok
    chunk = 2 * tok
    n_chunks = tokens // chunk

    def rows_of(t, i):
        return got[t, pl.ds(2 * i, 2)].reshape(chunk, width)

    arrived(0)

    def first(i, carry):
        rows = pl.ds(pl.multiple_of(i * chunk, chunk), chunk)
        keys = rows_of(0, i)
        p1 = dot(keys, wb[0])
        p3 = dot(keys, wb[2])
        sig = jax.nn.sigmoid(p1)
        act = p1 * sig
        hid[rows] = (act * p3).astype(BF16)
        t3[rows] = act
        t1[rows] = p3 * sig * (1.0 + p1 * (1.0 - sig))
        return carry

    lax.fori_loop(0, n_chunks, first, 0)
    for i in range(n_chunks):
        kt[:, i * chunk : (i + 1) * chunk] = rows_of(0, i).T
        ht[:, i * chunk : (i + 1) * chunk] = hid[i * chunk : (i + 1) * chunk].T
    arrived(1)

    def second(i, carry):
        rows = pl.ds(pl.multiple_of(i * chunk, chunk), chunk)
        back = dot_t(rows_of(1, i), wb[1])
        d1[rows] = (back * t1[rows]).astype(BF16)
        d3[rows] = (back * t3[rows]).astype(BF16)
        return carry

    lax.fori_loop(0, n_chunks, second, 0)

    def half_rows(cc):
        return pl.ds(pl.multiple_of(cc * half, half), half)

    def core_copy(m):
        return remote(cs.at[m], cr.at[m], c_ss.at[m], c_rs.at[m], core_dev)

    def gradient(m, left, right):
        cs[m] = dot(left[half_rows(1 - core)], right).astype(BF16)
        core_copy(m).start()
        own[m] = dot(left[half_rows(core)], right)

    def y_rows(j):
        return pl.ds(pl.multiple_of(j * block, block), block)

    def z_rows(j):
        return pl.ds(pl.multiple_of(j * 16 + (j // 2) * 8, 8), PIECE)

    def y_copy(m, j, src):
        return remote(ys.at[m, j], yr.at[m, src], y_ss.at[m, j], y_rs.at[m, src], y_dev(j))

    def z_copy(m, j, src):
        return remote(zs.at[m, j], zr.at[m, src], z_ss.at[m, j], z_rs.at[m, src], z_dev(j))

    def zg_copy(m, j, src):
        return remote(zg.at[m, src], zg.at[m, src], zg_ss.at[m, j], zg_rs.at[m, src], z_dev(j))

    def yg_copy(m, j, src):
        slot = x0.at[m, core, src]
        return remote(slot, slot, yg_ss.at[m, j], yg_rs.at[m, src], y_dev(j))

    def cg_copy(m, cc):
        slot = x0.at[m, cc]
        return remote(slot, slot, cg_ss.at[m], cg_rs.at[m], core_dev)

    def start_y(m):
        core_copy(m).wait()
        own[m] = own[m] + cr[m].astype(F32)
        for s in range(1, NY):
            j = (y + s) % NY
            ys[m, j] = own[m, y_rows(j)].astype(BF16)
            y_copy(m, j, y).start()

    def start_z(m):
        total = own[m, y_rows(y)]
        for s in range(1, NY):
            j = (y + s) % NY
            y_copy(m, j, y).wait_send()
            y_copy(m, j, j).wait_recv()
            total = total + yr[m, j].astype(F32)
        zq[m] = total
        for s in range(1, NZ):
            j = (z + s) % NZ
            zs[m, j] = zq[m, z_rows(j)].astype(BF16)
            z_copy(m, j, z).start()

    def start_zg(m):
        total = zq[m, z_rows(z)]
        for s in range(1, NZ):
            j = (z + s) % NZ
            z_copy(m, j, z).wait_send()
            z_copy(m, j, j).wait_recv()
            total = total + zr[m, j].astype(F32)
        zg[m, z] = total.astype(BF16)
        for s in range(1, NZ):
            zg_copy(m, (z + s) % NZ, z).start()

    def start_yg(m):
        for s in range(1, NZ):
            j = (z + s) % NZ
            zg_copy(m, j, z).wait_send()
            zg_copy(m, j, j).wait_recv()
        parts = [zg[m, j].astype(F32) for j in range(NZ)]
        whole = jnp.concatenate([parts[0][:16], parts[1], parts[2][:16], parts[3]], axis=0)
        x0[m, core, y] = whole.astype(BF16)
        for s in range(1, NY):
            yg_copy(m, (y + s) % NY, y).start()

    def start_cg(m):
        for s in range(1, NY):
            j = (y + s) % NY
            yg_copy(m, j, y).wait_send()
            yg_copy(m, j, j).wait_recv()
        cg_copy(m, core).start()

    def halves(fn):
        def step(i, carry):
            fn(i, pl.ds(pl.multiple_of(i * half, half), half))
            return carry

        lax.fori_loop(0, 2, step, 0)

    def ns_steps(m, w_index):
        cell = {}

        def grad_half(i):
            return x0[m, i].reshape(half, width)

        def grad_full():
            return x0[m].reshape(width, width)

        def square0():
            cg_copy(m, core).wait_send()
            cg_copy(m, 1 - core).wait_recv()
            total = jnp.zeros((1, 1), F32)
            for i in range(2):
                g = grad_half(i).astype(F32)
                total = total + jnp.sum(g * g, axis=(0, 1), keepdims=True)
            inv = 1.0 / (jnp.sqrt(total) + frob_eps)
            cell["inv"] = inv

            def fn(i, rows):
                xs[rows] = (dot_t(grad_half(i), grad_full()) * inv * inv).astype(BF16)

            halves(fn)

        def poly():
            def fn(i, rows):
                s = xs[rows]
                xm[rows] = (coeff_b * s.astype(F32) + coeff_c * dot(s, xs[...])).astype(BF16)

            halves(fn)

        def step0():
            inv = cell["inv"]

            def fn(i, rows):
                g = grad_half(i).astype(F32)
                x1[rows] = ((coeff_a * g + dot(xm[rows], grad_full())) * inv).astype(BF16)

            halves(fn)

        def square1():
            def fn(i, rows):
                xs[rows] = dot_t(x1[rows], x1[...]).astype(BF16)

            halves(fn)

        def step1():
            def fn(i, rows):
                new = (coeff_a * x1[rows].astype(F32) + dot(xm[rows], x1[...])).astype(BF16)
                u[m, rows] = (wf[w_index, rows] + step_size * new.astype(F32)).astype(BF16)

            halves(fn)

        return [square0, poly, step0, square1, poly, step1]

    gradient(0, kt, d3[...])
    gradient(1, kt, d1[...])
    start_y(0)
    gradient(2, ht, got[1].reshape(tokens, width))
    start_y(1)
    start_y(2)
    start_z(0)
    start_z(1)
    start_zg(0)
    start_z(2)
    start_zg(1)
    start_yg(0)
    start_zg(2)
    start_yg(1)
    start_cg(0)
    ns0 = ns_steps(0, 2)
    ns0[0]()
    start_yg(2)
    ns0[1]()
    ns0[2]()
    start_cg(1)
    ns0[3]()
    ns0[4]()
    start_cg(2)
    ns0[5]()
    for fn in ns_steps(1, 0):
        fn()

    arrived(2)

    def gate(i, carry):
        rows = pl.ds(pl.multiple_of(i * chunk, chunk), chunk)
        queries = rows_of(2, i)
        a = dot(queries, u[1])
        b = dot(queries, u[0])
        fw[rows] = (a * jax.nn.sigmoid(a) * b).astype(BF16)
        return carry

    lax.fori_loop(0, n_chunks, gate, 0)
    for fn in ns_steps(2, 1):
        fn()

    def o_copy(j, src):
        return remote(ob.at[j], orx.at[src], o_ss.at[j], o_rs.at[src], (j, me_c))

    mine = me_h // 2

    def finish(i):
        c = (mine + i) % n_chunks
        rows = pl.ds(pl.multiple_of(c * chunk, chunk), chunk)
        o = dot(fw[rows], u[2])
        o = o * lax.rsqrt(jnp.mean(o * o, axis=-1, keepdims=True) + epsilon)
        ob[pl.ds(2 * c, 2)] = o.astype(BF16).reshape(2, tok, width)
        return c

    def others(i, carry):
        c = finish(i)
        o_copy(2 * c, me_h).start()
        o_copy(2 * c + 1, me_h).start()
        return carry

    lax.fori_loop(1, n_chunks, others, 0)
    finish(0)
    twin = mine * 2 + (1 - me_h % 2)
    o_copy(twin, me_h).start()
    orx[me_h] = ob[me_h]

    def back(s, carry):
        j = head_peer(s)
        o_copy(j, me_h).wait_send()
        o_copy(j, j).wait_recv()
        return carry

    lax.fori_loop(1, nh, back, 0)
    for j in range(nh):
        out_ref[:, j * width : (j + 1) * width] = orx[j]


def per_device(queries, keys, values, rates, q_gain, k_gain, w_first, w_second, w_third):
    nh = rates.shape[1]
    tok, model = queries.shape
    width = model // nh
    tokens = nh * tok
    half, block = width // 2, width // 2 // NY
    vmem = pl.BlockSpec(memory_space=pltpu.VMEM)
    hbm = pl.BlockSpec(memory_space=pl.ANY)
    dma = pltpu.SemaphoreType.DMA
    return pl.pallas_call(
        functools.partial(kernel, nh),
        out_shape=jax.ShapeDtypeStruct((tok, model), BF16),
        in_specs=[vmem] * 6 + [hbm] * 3,
        out_specs=vmem,
        scratch_shapes=[
            pltpu.VMEM((3, nh, tok, width), BF16),
            pltpu.VMEM((3, nh, tok, width), BF16),
            pltpu.VMEM((3, width, width), F32),
            pltpu.VMEM((3, width, width), BF16),
            pltpu.VMEM((tokens, width), F32),
            pltpu.VMEM((tokens, width), F32),
            pltpu.VMEM((tokens, width), BF16),
            pltpu.VMEM((tokens, width), BF16),
            pltpu.VMEM((tokens, width), BF16),
            pltpu.VMEM((width, tokens), BF16),
            pltpu.VMEM((width, tokens), BF16),
            pltpu.VMEM((3, half, width), F32),
            pltpu.VMEM((3, half, width), BF16),
            pltpu.VMEM((3, half, width), BF16),
            pltpu.VMEM((3, NY, block, width), BF16),
            pltpu.VMEM((3, NY, block, width), BF16),
            pltpu.VMEM((3, block, width), F32),
            pltpu.VMEM((3, NZ, PIECE, width), BF16),
            pltpu.VMEM((3, NZ, PIECE, width), BF16),
            pltpu.VMEM((3, NZ, PIECE, width), BF16),
            pltpu.VMEM((3, 2, NY, block, width), BF16),
            pltpu.VMEM((width, width), BF16),
            pltpu.VMEM((width, width), BF16),
            pltpu.VMEM((width, width), BF16),
            pltpu.VMEM((3, width, width), BF16),
            pltpu.VMEM((tokens, width), BF16),
            pltpu.VMEM((nh, tok, width), BF16),
            pltpu.VMEM((nh, tok, width), BF16),
            dma((3,)),
            dma((3, nh)), dma((3, nh)),
            dma((3,)), dma((3,)),
            dma((3, NY)), dma((3, NY)),
            dma((3, NZ)), dma((3, NZ)),
            dma((3, NZ)), dma((3, NZ)),
            dma((3, NY)), dma((3, NY)),
            dma((3,)), dma((3,)),
            dma((nh,)), dma((nh,)),
        ],
        compiler_params=pltpu.CompilerParams(
            collective_id=0, has_side_effects=True, vmem_limit_bytes=58 * 2**20
        ),
        name="span",
    )(
        queries, keys, values, rates, q_gain.reshape(1, model), k_gain.reshape(1, model),
        w_first, w_second, w_third,
    )


def solution(mesh):
    return jax.shard_map(
        per_device,
        mesh=mesh,
        in_specs=(
            P(("head", "ctx"), None),
            P(("head", "ctx"), None),
            P(("head", "ctx"), None),
            P(("head", "ctx"), None),
            P(),
            P(),
            P("head", None, None),
            P("head", None, None),
            P("head", None, None),
        ),
        out_specs=P(("head", "ctx"), None),
        check_vma=False,
    )
```

```python
import functools

import jax
import jax.numpy as jnp
from jax import lax
from jax.experimental import pallas as pl
from jax.experimental.pallas import tpu as pltpu
from jax.sharding import PartitionSpec as P

MESH = pl.DeviceIdType.MESH
F32 = jnp.float32
BF16 = jnp.bfloat16

epsilon = 1e-06
frob_eps = 1e-07
coeff_a = 3.4445
coeff_b = -4.775
coeff_c = 2.0315
step_size = 1.0

NY, NZ = 4, 4
VMEM_LIMIT = 54 * 2**20
PIECE = 24

ORDER = (
    "g0", "g1", "g2", "y0", "y1", "g3", "y2", "y3", "g4", "z0", "y4", "g5", "y5", "z1", "zg0",
    "z2", "zg1", "z3", "yg0", "zg2", "yg1", "z4", "zg3", "yg2", "z5", "c0", "c1", "zg4", "yg3",
    "n0", "n0", "zg5", "n0", "c2", "n0", "yg4", "c3", "n0", "n0", "n1", "yg5", "n1", "n1", "n1",
    "n1", "n1", "c4", "c5",
)


def dot(a, b):
    return jnp.dot(a, b, preferred_element_type=F32)


def dot_t(a, b):
    return lax.dot_general(a, b, (((1,), (1,)), ((), ())), preferred_element_type=F32)


def kernel(
    nh,
    q_hbm, k_hbm, v_hbm, r_hbm, qg_hbm, kg_hbm, w1_hbm, w2_hbm, w3_hbm,
    out,
    q_ref, k_ref, v_ref, r_ref, qg_ref, kg_ref, rb,
    sent, got, wf, wb, t1, t3, hid, d1, d3, kt, ht, e_ref,
    own, cs, cr, ys, yr, zq, zs, zr, zg, x0, xs, xm, x1, u, fw, ob,
    in_sem, a_ss, a_rs, c_ss, c_rs, y_ss, y_rs, z_ss, z_rs,
    zg_ss, zg_rs, yg_ss, yg_rs, cg_ss, cg_rs, o_ss, o_rs,
):
    me_h = lax.axis_index("head")
    me_c = lax.axis_index("ctx")
    y = me_c // (2 * NZ)
    z = (me_c // 2) % NZ
    core = me_c % 2
    tok, width = sent.shape[2], sent.shape[3]
    half = width // 2
    block = half // NY

    def head_peer(s):
        return (me_h + s) % nh

    def ctx_of(yy, zz, cc):
        return (yy * NZ + zz) * 2 + cc

    def z_dev(zz):
        return (me_h, ctx_of(y, zz, core))

    def y_dev(yy):
        return (me_h, ctx_of(yy, z, core))

    core_dev = (me_h, ctx_of(y, z, 1 - core))

    def remote(src, dst, ss, rs, dev):
        return pltpu.make_async_remote_copy(
            src_ref=src, dst_ref=dst, send_sem=ss, recv_sem=rs, device_id=dev, device_id_type=MESH
        )

    barrier = pltpu.get_barrier_semaphore()

    def greet(dev):
        pl.semaphore_signal(barrier, inc=1, device_id=dev, device_id_type=MESH)

    for s in range(1, nh):
        greet((head_peer(s), me_c))
    for s in range(1, NY):
        greet(y_dev((y + s) % NY))
    for s in range(1, NZ):
        greet(z_dev((z + s) % NZ))
    greet(core_dev)

    loads = [
        pltpu.make_async_copy(src, dst, in_sem.at[i])
        for i, (src, dst) in enumerate(
            [
                (k_hbm, k_ref), (kg_hbm, kg_ref), (v_hbm, v_ref), (r_hbm, r_ref),
                (q_hbm, q_ref), (qg_hbm, qg_ref),
                (w1_hbm.at[0], wf.at[0]), (w3_hbm.at[0], wf.at[2]), (w2_hbm.at[0], wf.at[1]),
            ]
        )
    ]
    for copy in loads:
        copy.start()

    def cols(j):
        return pl.ds(pl.multiple_of(j * width, 128), width)

    def send(t, fn):
        def step(s, carry):
            j = head_peer(s)
            sent[t, j] = fn(j)
            remote(
                sent.at[t, j], got.at[t, me_h], a_ss.at[t, j], a_rs.at[t, me_h], (j, me_c)
            ).start()
            return carry

        lax.fori_loop(1, nh, step, 0)
        got[t, me_h] = fn(me_h)

    def factor_of(x_ref):
        total = jnp.zeros((tok, 1), F32)
        for j in range(nh):
            x = x_ref[:, j * width : (j + 1) * width].astype(F32)
            total = total + jnp.sum(x * x, axis=-1, keepdims=True)
        return lax.rsqrt(total / (nh * width) + epsilon)

    def normalized(x_ref, g_ref, factor):
        return lambda j: (x_ref[:, cols(j)].astype(F32) * factor * g_ref[:, cols(j)]).astype(BF16)

    def arrived(t):
        def step(s, carry):
            j = head_peer(s)
            remote(
                sent.at[t, j], got.at[t, j], a_ss.at[t, j], a_rs.at[t, j], (j, me_c)
            ).wait()
            return carry

        lax.fori_loop(1, nh, step, 0)

    def rated(j):
        wide = jnp.concatenate([rb[j]] * (width // 128), axis=-1)
        return (wide * v_ref[:, cols(j)].astype(F32)).astype(BF16)

    loads[0].wait()
    loads[1].wait()
    factor = factor_of(k_ref)
    pl.semaphore_wait(barrier, nh - 1 + NY - 1 + NZ - 1 + 1)
    send(0, normalized(k_ref, kg_ref, factor))
    loads[2].wait()
    loads[3].wait()
    rate = r_ref[...].astype(F32).T
    for j in range(nh):
        rb[j] = jnp.broadcast_to(rate[:, j : j + 1], (tok, 128))
    send(1, rated)
    loads[4].wait()
    loads[5].wait()
    send(2, normalized(q_ref, qg_ref, factor_of(q_ref)))
    for i in range(3):
        loads[6 + i].wait()
    for i in range(3):
        wb[i] = wf[i].astype(BF16)

    tokens = nh * tok

    def whole(t):
        return got[t].reshape(tokens, width)

    arrived(0)
    p1 = dot(whole(0), wb[0])
    p3 = dot(whole(0), wb[2])
    sig = jax.nn.sigmoid(p1)
    act = p1 * sig
    hid[...] = (act * p3).astype(BF16)
    t3[...] = act
    t1[...] = p3 * sig * (1.0 + p1 * (1.0 - sig))
    kt[...] = whole(0).T
    ht[...] = hid[...].T
    arrived(1)
    e_ref[...] = whole(1)
    back = dot_t(whole(1), wb[1])
    d3[...] = (back * t3[...]).astype(BF16)
    d1[...] = (back * t1[...]).astype(BF16)

    cut = 3 * 128
    chunks = [(m, c) for m in range(3) for c in (slice(0, cut), slice(cut, width))]

    def half_rows(cc):
        return pl.ds(pl.multiple_of(cc * half, half), half)

    def core_copy(q):
        m, c = chunks[q]
        return remote(cs.at[m, :, c], cr.at[m, :, c], c_ss.at[q], c_rs.at[q], core_dev)

    def gradient(q, left, right):
        m, c = chunks[q]
        cs[m, :, c] = dot(left[half_rows(1 - core)], right[:, c]).astype(BF16)
        core_copy(q).start()
        own[m, :, c] = dot(left[half_rows(core)], right[:, c])

    def y_rows(j):
        return pl.ds(pl.multiple_of(j * block, 8), block)

    def z_rows(j):
        return pl.ds(pl.multiple_of(j * 16 + (j // 2) * 8, 8), PIECE)

    def y_copy(q, j, src):
        m, c = chunks[q]
        return remote(
            ys.at[m, j, :, c], yr.at[m, src, :, c], y_ss.at[q, j], y_rs.at[q, src], y_dev(j)
        )

    def z_copy(q, j, src):
        m, c = chunks[q]
        return remote(
            zs.at[m, j, :, c], zr.at[m, src, :, c], z_ss.at[q, j], z_rs.at[q, src], z_dev(j)
        )

    def zg_copy(q, j, src):
        m, c = chunks[q]
        slot = zg.at[m, src, :, c]
        return remote(slot, slot, zg_ss.at[q, j], zg_rs.at[q, src], z_dev(j))

    def yg_copy(q, j, src):
        m, c = chunks[q]
        slot = x0.at[m, core, src, :, c]
        return remote(slot, slot, yg_ss.at[q, j], yg_rs.at[q, src], y_dev(j))

    def cg_copy(q, cc, j):
        m, c = chunks[q]
        slot = x0.at[m, cc, j, :, c]
        return remote(slot, slot, cg_ss.at[q, j], cg_rs.at[q, j], core_dev)

    def start_y(q):
        m, c = chunks[q]
        core_copy(q).wait()
        own[m, :, c] = own[m, :, c] + cr[m, :, c].astype(F32)
        for s in (2, 1, 3):
            j = (y + s) % NY
            ys[m, j, :, c] = own[m, y_rows(j), c].astype(BF16)
            y_copy(q, j, y).start()

    def start_z(q):
        m, c = chunks[q]
        total = own[m, y_rows(y), c]
        for s in range(1, NY):
            j = (y + s) % NY
            y_copy(q, j, y).wait_send()
            y_copy(q, j, j).wait_recv()
            total = total + yr[m, j, :, c].astype(F32)
        zq[m, :, c] = total
        for s in range(1, NZ):
            j = (z + s) % NZ
            zs[m, j, :, c] = zq[m, z_rows(j), c].astype(BF16)
            z_copy(q, j, z).start()

    def start_zg(q):
        m, c = chunks[q]
        total = zq[m, z_rows(z), c]
        for s in range(1, NZ):
            j = (z + s) % NZ
            z_copy(q, j, z).wait_send()
            z_copy(q, j, j).wait_recv()
            total = total + zr[m, j, :, c].astype(F32)
        zg[m, z, :, c] = total.astype(BF16)
        for s in range(1, NZ):
            zg_copy(q, (z + s) % NZ, z).start()

    def start_yg(q):
        m, c = chunks[q]
        for s in range(1, NZ):
            j = (z + s) % NZ
            zg_copy(q, j, z).wait_send()
            zg_copy(q, j, j).wait_recv()
        parts = [zg[m, j, :, c].astype(F32) for j in range(NZ)]
        total = jnp.concatenate([parts[0][:16], parts[1], parts[2][:16], parts[3]], axis=0)
        x0[m, core, y, :, c] = total.astype(BF16)
        for s in (2, 1, 3):
            yg_copy(q, (y + s) % NY, y).start()
        cg_copy(q, core, y).start()

    def start_cg(q):
        for s in (1, 3, 2):
            j = (y + s) % NY
            yg_copy(q, j, y).wait_send()
            yg_copy(q, j, j).wait_recv()
            cg_copy(q, core, j).start()

    def gathered(m):
        for q in (2 * m, 2 * m + 1):
            for j in range(NY):
                cg_copy(q, core, j).wait_send()
                cg_copy(q, 1 - core, j).wait_recv()

    def ns_steps(m, w_index):
        cell = {}

        def grad():
            return x0[m].reshape(width, width)

        def square0():
            gathered(m)
            g = grad().astype(F32)
            inv = 1.0 / (jnp.sqrt(jnp.sum(g * g, axis=(0, 1), keepdims=True)) + frob_eps)
            cell["inv"] = inv
            xs[...] = (dot_t(grad(), grad()) * inv * inv).astype(BF16)

        def poly():
            s = xs[...]
            xm[...] = (coeff_b * s.astype(F32) + coeff_c * dot(s, s)).astype(BF16)

        def step0():
            g = grad()
            x1[...] = ((coeff_a * g.astype(F32) + dot(xm[...], g)) * cell["inv"]).astype(BF16)

        def square1():
            xs[...] = dot_t(x1[...], x1[...]).astype(BF16)

        def step1():
            new = (coeff_a * x1[...].astype(F32) + dot(xm[...], x1[...])).astype(BF16)
            u[m] = (wf[w_index] + step_size * new.astype(F32)).astype(BF16)

        return [square0, poly, step0, square1, poly, step1]

    factors = ((kt, d3), (kt, d1), (ht, e_ref))
    iterations = [iter(ns_steps(0, 2)), iter(ns_steps(1, 0))]

    def start_g(q):
        gradient(q, *factors[q // 2])

    stages = {
        "g": start_g, "y": start_y, "z": start_z, "zg": start_zg, "yg": start_yg, "c": start_cg,
    }
    for event in ORDER:
        name, index = event[:-1], int(event[-1])
        if name == "n":
            next(iterations[index])()
        else:
            stages[name](index)

    arrived(2)
    a = dot(whole(2), u[1])
    b = dot(whole(2), u[0])
    fw[...] = (a * jax.nn.sigmoid(a) * b).astype(BF16)
    for fn in ns_steps(2, 1):
        fn()

    def o_copy(j, src):
        return remote(ob.at[j], out.at[src], o_ss.at[j], o_rs.at[src], (j, me_c))

    chunk = 2 * tok
    n_chunks = tokens // chunk
    mine = me_h // 2

    def finish(i):
        c = (mine + i) % n_chunks
        rows = pl.ds(pl.multiple_of(c * chunk, chunk), chunk)
        o = dot(fw[rows], u[2])
        o = o * lax.rsqrt(jnp.mean(o * o, axis=-1, keepdims=True) + epsilon)
        ob[pl.ds(2 * c, 2)] = o.astype(BF16).reshape(2, tok, width)
        return c

    def others(i, carry):
        c = finish(i)
        o_copy(2 * c, me_h).start()
        o_copy(2 * c + 1, me_h).start()
        return carry

    lax.fori_loop(1, n_chunks, others, 0)
    finish(0)
    o_copy(mine * 2 + (1 - me_h % 2), me_h).start()
    keep = pltpu.make_async_copy(ob.at[me_h], out.at[me_h], in_sem.at[0])
    keep.start()

    def returned(s, carry):
        j = head_peer(s)
        o_copy(j, me_h).wait_send()
        o_copy(j, j).wait_recv()
        return carry

    lax.fori_loop(1, nh, returned, 0)
    keep.wait()


def per_device(queries, keys, values, rates, q_gain, k_gain, w_first, w_second, w_third):
    nh = rates.shape[1]
    tok, model = queries.shape
    width = model // nh
    tokens = nh * tok
    half = width // 2
    block = half // NY
    hbm = pl.BlockSpec(memory_space=pl.ANY)

    def dma(*shape):
        return pltpu.SemaphoreType.DMA(shape)

    out = pl.pallas_call(
        functools.partial(kernel, nh),
        out_shape=jax.ShapeDtypeStruct((nh, tok, width), BF16),
        in_specs=[hbm] * 9,
        out_specs=hbm,
        scratch_shapes=[
            pltpu.VMEM((tok, model), BF16),
            pltpu.VMEM((tok, model), BF16),
            pltpu.VMEM((tok, model), BF16),
            pltpu.VMEM((nh, tok), BF16),
            pltpu.VMEM((1, model), F32),
            pltpu.VMEM((1, model), F32),
            pltpu.VMEM((nh, tok, 128), F32),
            pltpu.VMEM((3, nh, tok, width), BF16),
            pltpu.VMEM((3, nh, tok, width), BF16),
            pltpu.VMEM((3, width, width), F32),
            pltpu.VMEM((3, width, width), BF16),
            pltpu.VMEM((tokens, width), F32),
            pltpu.VMEM((tokens, width), F32),
            pltpu.VMEM((tokens, width), BF16),
            pltpu.VMEM((tokens, width), BF16),
            pltpu.VMEM((tokens, width), BF16),
            pltpu.VMEM((width, tokens), BF16),
            pltpu.VMEM((width, tokens), BF16),
            pltpu.VMEM((tokens, width), BF16),
            pltpu.VMEM((3, half, width), F32),
            pltpu.VMEM((3, half, width), BF16),
            pltpu.VMEM((3, half, width), BF16),
            *[pltpu.VMEM((3, NY, block, width), BF16)] * 2,
            pltpu.VMEM((3, block, width), F32),
            pltpu.VMEM((3, NZ, PIECE, width), BF16),
            pltpu.VMEM((3, NZ, PIECE, width), BF16),
            pltpu.VMEM((3, NZ, PIECE, width), BF16),
            pltpu.VMEM((3, 2, NY, block, width), BF16),
            pltpu.VMEM((width, width), BF16),
            pltpu.VMEM((width, width), BF16),
            pltpu.VMEM((width, width), BF16),
            pltpu.VMEM((3, width, width), BF16),
            pltpu.VMEM((tokens, width), BF16),
            pltpu.VMEM((nh, tok, width), BF16),
            dma(9),
            dma(3, nh), dma(3, nh),
            dma(6), dma(6),
            *[dma(6, NY)] * 2,
            *[dma(6, NZ)] * 4,
            *[dma(6, NY)] * 4,
            dma(nh), dma(nh),
        ],
        compiler_params=pltpu.CompilerParams(
            collective_id=0, has_side_effects=True, vmem_limit_bytes=VMEM_LIMIT
        ),
        name="span",
    )(
        queries, keys, values, rates.T, q_gain.reshape(1, model), k_gain.reshape(1, model),
        w_first, w_second, w_third,
    )
    return out.transpose(1, 0, 2).reshape(tok, model)


def solution(mesh):
    return jax.shard_map(
        per_device,
        mesh=mesh,
        in_specs=(
            P(("head", "ctx"), None),
            P(("head", "ctx"), None),
            P(("head", "ctx"), None),
            P(("head", "ctx"), None),
            P(),
            P(),
            P("head", None, None),
            P("head", None, None),
            P("head", None, None),
        ),
        out_specs=P(("head", "ctx"), None),
        check_vma=False,
    )
```

```python
import functools

import jax
import jax.numpy as jnp
from jax import lax
from jax.experimental import pallas as pl
from jax.experimental.pallas import tpu as pltpu
from jax.sharding import PartitionSpec as P

MESH = pl.DeviceIdType.MESH
F32 = jnp.float32
BF16 = jnp.bfloat16

epsilon = 1e-06
frob_eps = 1e-07
coeff_a = 3.4445
coeff_b = -4.775
coeff_c = 2.0315
step_size = 1.0

NY, NZ = 4, 4
VMEM_LIMIT = 54 * 2**20
CUTS = (0, 2, 5)
PIECE = 24

ORDER = (
    "g0", "g1", "g2", "y0", "y1", "g3", "g4", "z0", "y3", "y2", "y4", "z1", "g5", "zg0", "z3",
    "y5", "zg1", "z2", "z4", "yg0", "zg3", "z5", "yg1", "zg2", "zg4", "c0", "yg3", "zg5", "c1",
    "yg2", "n0", "yg4", "n0", "n0", "n0", "c3", "yg5", "c2", "n0", "n0", "n1", "n1", "n1", "n1",
    "n1", "n1", "c5", "c4",
)


def dot(a, b):
    return jnp.dot(a, b, preferred_element_type=F32)


def dot_t(a, b):
    return lax.dot_general(a, b, (((1,), (1,)), ((), ())), preferred_element_type=F32)


def kernel(
    nh,
    q_hbm, k_hbm, v_hbm, r_hbm, qg_hbm, kg_hbm, w1_hbm, w2_hbm, w3_hbm,
    out,
    q_ref, k_ref, v_ref, r_ref, qg_ref, kg_ref, rb,
    sent, got, wf, wb, t1, t3, hid, d1, d3, kt, ht, e_ref,
    own, cs, cr, ys, yr, zq, zs, zr, zg, x0, xs, xm, x1, u, fw, ob,
    in_sem, a_ss, a_rs, c_ss, c_rs, y_ss, y_rs, z_ss, z_rs,
    zg_ss, zg_rs, yg_ss, yg_rs, cg_ss, cg_rs, o_ss, o_rs,
):
    me_h = lax.axis_index("head")
    me_c = lax.axis_index("ctx")
    y = me_c // (2 * NZ)
    z = (me_c // 2) % NZ
    core = me_c % 2
    tok, width = sent.shape[2], sent.shape[3]
    half = width // 2
    block = half // NY

    def head_peer(s):
        return (me_h + s) % nh

    def ctx_of(yy, zz, cc):
        return (yy * NZ + zz) * 2 + cc

    def z_dev(zz):
        return (me_h, ctx_of(y, zz, core))

    def y_dev(yy):
        return (me_h, ctx_of(yy, z, core))

    core_dev = (me_h, ctx_of(y, z, 1 - core))

    def remote(src, dst, ss, rs, dev):
        return pltpu.make_async_remote_copy(
            src_ref=src, dst_ref=dst, send_sem=ss, recv_sem=rs, device_id=dev, device_id_type=MESH
        )

    barrier = pltpu.get_barrier_semaphore()

    def greet(dev):
        pl.semaphore_signal(barrier, inc=1, device_id=dev, device_id_type=MESH)

    for s in range(1, nh):
        greet((head_peer(s), me_c))
    for s in range(1, NY):
        greet(y_dev((y + s) % NY))
    for s in range(1, NZ):
        greet(z_dev((z + s) % NZ))
    greet(core_dev)

    loads = [
        pltpu.make_async_copy(src, dst, in_sem.at[i])
        for i, (src, dst) in enumerate(
            [
                (k_hbm, k_ref), (kg_hbm, kg_ref), (v_hbm, v_ref), (r_hbm, r_ref),
                (q_hbm, q_ref), (qg_hbm, qg_ref),
                (w1_hbm.at[0], wf.at[0]), (w3_hbm.at[0], wf.at[2]), (w2_hbm.at[0], wf.at[1]),
            ]
        )
    ]
    for copy in loads:
        copy.start()

    def cols(j):
        return pl.ds(pl.multiple_of(j * width, 128), width)

    def send(t, fn):
        def step(s, carry):
            j = head_peer(s)
            sent[t, j] = fn(j)
            remote(
                sent.at[t, j], got.at[t, me_h], a_ss.at[t, j], a_rs.at[t, me_h], (j, me_c)
            ).start()
            return carry

        lax.fori_loop(1, nh, step, 0)
        got[t, me_h] = fn(me_h)

    def factor_of(x_ref):
        total = jnp.zeros((tok, 1), F32)
        for j in range(nh):
            x = x_ref[:, j * width : (j + 1) * width].astype(F32)
            total = total + jnp.sum(x * x, axis=-1, keepdims=True)
        return lax.rsqrt(total / (nh * width) + epsilon)

    def normalized(x_ref, g_ref, factor):
        return lambda j: (x_ref[:, cols(j)].astype(F32) * factor * g_ref[:, cols(j)]).astype(BF16)

    def arrived(t):
        def step(s, carry):
            j = head_peer(s)
            remote(
                sent.at[t, j], got.at[t, j], a_ss.at[t, j], a_rs.at[t, j], (j, me_c)
            ).wait_recv()
            return carry

        lax.fori_loop(1, nh, step, 0)

    def rated(j):
        wide = jnp.concatenate([rb[j]] * (width // 128), axis=-1)
        return (wide * v_ref[:, cols(j)].astype(F32)).astype(BF16)

    loads[0].wait()
    loads[1].wait()
    factor = factor_of(k_ref)
    pl.semaphore_wait(barrier, nh - 1 + NY - 1 + NZ - 1 + 1)
    send(0, normalized(k_ref, kg_ref, factor))
    loads[2].wait()
    loads[3].wait()
    rate = r_ref[...].astype(F32).T
    for j in range(nh):
        rb[j] = jnp.broadcast_to(rate[:, j : j + 1], (tok, 128))
    send(1, rated)
    loads[4].wait()
    loads[5].wait()
    send(2, normalized(q_ref, qg_ref, factor_of(q_ref)))
    for i in range(3):
        loads[6 + i].wait()
    for i in range(3):
        wb[i] = wf[i].astype(BF16)

    tokens = nh * tok

    def whole(t):
        return got[t].reshape(tokens, width)

    arrived(0)
    p1 = dot(whole(0), wb[0])
    p3 = dot(whole(0), wb[2])
    sig = jax.nn.sigmoid(p1)
    act = p1 * sig
    hid[...] = (act * p3).astype(BF16)
    t3[...] = act
    t1[...] = p3 * sig * (1.0 + p1 * (1.0 - sig))
    kt[...] = whole(0).T
    ht[...] = hid[...].T
    arrived(1)
    e_ref[...] = whole(1)
    back = dot_t(whole(1), wb[1])
    d3[...] = (back * t3[...]).astype(BF16)
    d1[...] = (back * t1[...]).astype(BF16)

    chunks = [(m, slice(a * 128, b * 128)) for m in range(3) for a, b in zip(CUTS, CUTS[1:])]
    per_matrix = len(CUTS) - 1

    def half_rows(cc):
        return pl.ds(pl.multiple_of(cc * half, half), half)

    def core_copy(q):
        m, c = chunks[q]
        return remote(cs.at[m, :, c], cr.at[m, :, c], c_ss.at[q], c_rs.at[q], core_dev)

    def gradient(q, left, right):
        m, c = chunks[q]
        cs[m, :, c] = dot(left[half_rows(1 - core)], right[:, c]).astype(BF16)
        core_copy(q).start()
        own[m, :, c] = dot(left[half_rows(core)], right[:, c])

    def y_rows(j):
        return pl.ds(pl.multiple_of(j * block, 8), block)

    def z_rows(j):
        return pl.ds(pl.multiple_of(j * 16 + (j // 2) * 8, 8), PIECE)

    def y_copy(q, j, src):
        m, c = chunks[q]
        return remote(
            ys.at[m, j, :, c], yr.at[m, src, :, c], y_ss.at[q, j], y_rs.at[q, src], y_dev(j)
        )

    def z_copy(q, j, src):
        m, c = chunks[q]
        return remote(
            zs.at[m, j, :, c], zr.at[m, src, :, c], z_ss.at[q, j], z_rs.at[q, src], z_dev(j)
        )

    def zg_copy(q, j, src):
        m, c = chunks[q]
        slot = zg.at[m, src, :, c]
        return remote(slot, slot, zg_ss.at[q, j], zg_rs.at[q, src], z_dev(j))

    def yg_copy(q, j, src):
        m, c = chunks[q]
        slot = x0.at[m, core, src, :, c]
        return remote(slot, slot, yg_ss.at[q, j], yg_rs.at[q, src], y_dev(j))

    def cg_copy(q, cc, j):
        m, c = chunks[q]
        slot = x0.at[m, cc, j, :, c]
        return remote(slot, slot, cg_ss.at[q, j], cg_rs.at[q, j], core_dev)

    def pair_sum(q, j):
        m, c = chunks[q]
        return own[m, y_rows(j), c] + cr[m, pl.ds(pl.multiple_of(j * block, 16), block), c].astype(F32)

    def start_y(q):
        m, c = chunks[q]
        core_copy(q).wait_recv()
        for s in (2, 1, 3):
            j = (y + s) % NY
            ys[m, j, :, c] = pair_sum(q, j).astype(BF16)
            y_copy(q, j, y).start()

    def start_z(q):
        m, c = chunks[q]
        total = pair_sum(q, y)
        for s in range(1, NY):
            j = (y + s) % NY
            y_copy(q, j, j).wait_recv()
            total = total + yr[m, j, :, c].astype(F32)
        zq[m, :, c] = total
        for s in range(1, NZ):
            j = (z + s) % NZ
            zs[m, j, :, c] = zq[m, z_rows(j), c].astype(BF16)
            z_copy(q, j, z).start()

    def start_zg(q):
        m, c = chunks[q]
        total = zq[m, z_rows(z), c]
        for s in range(1, NZ):
            j = (z + s) % NZ
            z_copy(q, j, j).wait_recv()
            total = total + zr[m, j, :, c].astype(F32)
        zg[m, z, :, c] = total.astype(BF16)
        for s in range(1, NZ):
            zg_copy(q, (z + s) % NZ, z).start()

    def start_yg(q):
        m, c = chunks[q]
        for s in range(1, NZ):
            j = (z + s) % NZ
            zg_copy(q, j, j).wait_recv()
        parts = [zg[m, j, :, c].astype(F32) for j in range(NZ)]
        total = jnp.concatenate([parts[0][:16], parts[1], parts[2][:16], parts[3]], axis=0)
        x0[m, core, y, :, c] = total.astype(BF16)
        for s in (2, 1, 3):
            yg_copy(q, (y + s) % NY, y).start()
        cg_copy(q, core, y).start()

    def start_cg(q):
        for s in (1, 3, 2):
            j = (y + s) % NY
            yg_copy(q, j, j).wait_recv()
            cg_copy(q, core, j).start()

    def gathered(m):
        for q in range(per_matrix * m, per_matrix * (m + 1)):
            for j in range(NY):
                cg_copy(q, 1 - core, j).wait_recv()

    def ns_steps(m, w_index):
        cell = {}

        def grad():
            return x0[m].reshape(width, width)

        def square0():
            gathered(m)
            g = grad().astype(F32)
            inv = 1.0 / (jnp.sqrt(jnp.sum(g * g, axis=(0, 1), keepdims=True)) + frob_eps)
            cell["inv"] = inv
            xs[...] = (dot_t(grad(), grad()) * inv * inv).astype(BF16)

        def poly():
            s = xs[...]
            xm[...] = (coeff_b * s.astype(F32) + coeff_c * dot(s, s)).astype(BF16)

        def step0():
            g = grad()
            x1[...] = ((coeff_a * g.astype(F32) + dot(xm[...], g)) * cell["inv"]).astype(BF16)

        def square1():
            xs[...] = dot_t(x1[...], x1[...]).astype(BF16)

        def step1():
            new = (coeff_a * x1[...].astype(F32) + dot(xm[...], x1[...])).astype(BF16)
            u[m] = (wf[w_index] + step_size * new.astype(F32)).astype(BF16)

        return [square0, poly, step0, square1, poly, step1]

    factors = ((kt, d3), (kt, d1), (ht, e_ref))
    iterations = [iter(ns_steps(0, 2)), iter(ns_steps(1, 0))]

    def start_g(q):
        gradient(q, *factors[q // per_matrix])

    stages = {
        "g": start_g, "y": start_y, "z": start_z, "zg": start_zg, "yg": start_yg, "c": start_cg,
    }
    for event in ORDER:
        name, index = event[:-1], int(event[-1])
        if name == "n":
            next(iterations[index])()
        else:
            stages[name](index)

    arrived(2)
    a = dot(whole(2), u[1])
    b = dot(whole(2), u[0])
    fw[...] = (a * jax.nn.sigmoid(a) * b).astype(BF16)
    for fn in ns_steps(2, 1):
        fn()

    def o_copy(j, src):
        return remote(ob.at[j], out.at[src], o_ss.at[j], o_rs.at[src], (j, me_c))

    chunk = 2 * tok
    n_chunks = tokens // chunk
    mine = me_h // 2

    def finish(i):
        c = (mine + i) % n_chunks
        rows = pl.ds(pl.multiple_of(c * chunk, chunk), chunk)
        o = dot(fw[rows], u[2])
        o = o * lax.rsqrt(jnp.mean(o * o, axis=-1, keepdims=True) + epsilon)
        ob[pl.ds(2 * c, 2)] = o.astype(BF16).reshape(2, tok, width)
        return c

    def others(i, carry):
        c = finish(i)
        o_copy(2 * c, me_h).start()
        o_copy(2 * c + 1, me_h).start()
        return carry

    lax.fori_loop(1, n_chunks, others, 0)
    finish(0)
    o_copy(mine * 2 + (1 - me_h % 2), me_h).start()
    keep = pltpu.make_async_copy(ob.at[me_h], out.at[me_h], in_sem.at[0])
    keep.start()

    for q in range(len(chunks)):
        core_copy(q).wait_send()
        for s in range(1, NY):
            y_copy(q, (y + s) % NY, y).wait_send()
            yg_copy(q, (y + s) % NY, y).wait_send()
        for s in range(1, NZ):
            z_copy(q, (z + s) % NZ, z).wait_send()
            zg_copy(q, (z + s) % NZ, z).wait_send()
        for j in range(NY):
            cg_copy(q, core, j).wait_send()

    def returned(s, carry):
        j = head_peer(s)
        for t in range(3):
            remote(
                sent.at[t, j], got.at[t, j], a_ss.at[t, j], a_rs.at[t, j], (j, me_c)
            ).wait_send()
        o_copy(j, me_h).wait_send()
        o_copy(j, j).wait_recv()
        return carry

    lax.fori_loop(1, nh, returned, 0)
    keep.wait()


def per_device(queries, keys, values, rates, q_gain, k_gain, w_first, w_second, w_third):
    nh = rates.shape[1]
    tok, model = queries.shape
    width = model // nh
    tokens = nh * tok
    half = width // 2
    block = half // NY
    hbm = pl.BlockSpec(memory_space=pl.ANY)

    def dma(*shape):
        return pltpu.SemaphoreType.DMA(shape)

    out = pl.pallas_call(
        functools.partial(kernel, nh),
        out_shape=jax.ShapeDtypeStruct((nh, tok, width), BF16),
        in_specs=[hbm] * 9,
        out_specs=hbm,
        scratch_shapes=[
            pltpu.VMEM((tok, model), BF16),
            pltpu.VMEM((tok, model), BF16),
            pltpu.VMEM((tok, model), BF16),
            pltpu.VMEM((nh, tok), BF16),
            pltpu.VMEM((1, model), F32),
            pltpu.VMEM((1, model), F32),
            pltpu.VMEM((nh, tok, 128), F32),
            pltpu.VMEM((3, nh, tok, width), BF16),
            pltpu.VMEM((3, nh, tok, width), BF16),
            pltpu.VMEM((3, width, width), F32),
            pltpu.VMEM((3, width, width), BF16),
            pltpu.VMEM((tokens, width), F32),
            pltpu.VMEM((tokens, width), F32),
            pltpu.VMEM((tokens, width), BF16),
            pltpu.VMEM((tokens, width), BF16),
            pltpu.VMEM((tokens, width), BF16),
            pltpu.VMEM((width, tokens), BF16),
            pltpu.VMEM((width, tokens), BF16),
            pltpu.VMEM((tokens, width), BF16),
            pltpu.VMEM((3, half, width), F32),
            pltpu.VMEM((3, half, width), BF16),
            pltpu.VMEM((3, half, width), BF16),
            *[pltpu.VMEM((3, NY, block, width), BF16)] * 2,
            pltpu.VMEM((3, block, width), F32),
            pltpu.VMEM((3, NZ, PIECE, width), BF16),
            pltpu.VMEM((3, NZ, PIECE, width), BF16),
            pltpu.VMEM((3, NZ, PIECE, width), BF16),
            pltpu.VMEM((3, 2, NY, block, width), BF16),
            pltpu.VMEM((width, width), BF16),
            pltpu.VMEM((width, width), BF16),
            pltpu.VMEM((width, width), BF16),
            pltpu.VMEM((3, width, width), BF16),
            pltpu.VMEM((tokens, width), BF16),
            pltpu.VMEM((nh, tok, width), BF16),
            dma(9),
            dma(3, nh), dma(3, nh),
            dma(6), dma(6),
            *[dma(6, NY)] * 2,
            *[dma(6, NZ)] * 4,
            *[dma(6, NY)] * 4,
            dma(nh), dma(nh),
        ],
        compiler_params=pltpu.CompilerParams(
            collective_id=0, has_side_effects=True, vmem_limit_bytes=VMEM_LIMIT
        ),
        name="span",
    )(
        queries, keys, values, rates.T, q_gain.reshape(1, model), k_gain.reshape(1, model),
        w_first, w_second, w_third,
    )
    return out.transpose(1, 0, 2).reshape(tok, model)


def solution(mesh):
    return jax.shard_map(
        per_device,
        mesh=mesh,
        in_specs=(
            P(("head", "ctx"), None),
            P(("head", "ctx"), None),
            P(("head", "ctx"), None),
            P(("head", "ctx"), None),
            P(),
            P(),
            P("head", None, None),
            P("head", None, None),
            P("head", None, None),
        ),
        out_specs=P(("head", "ctx"), None),
        check_vma=False,
    )
```

```python
import functools

import jax
import jax.numpy as jnp
from jax import lax
from jax.experimental import pallas as pl
from jax.experimental.pallas import tpu as pltpu
from jax.sharding import PartitionSpec as P

MESH = pl.DeviceIdType.MESH
F32 = jnp.float32
BF16 = jnp.bfloat16

epsilon = 1e-06
frob_eps = 1e-07
coeff_a = 3.4445
coeff_b = -4.775
coeff_c = 2.0315
step_size = 1.0

NY, NZ = 4, 4
VMEM_LIMIT = 54 * 2**20
CUTS = (0, 2, 5)
PIECE = 24

ORDER = (
    "g0", "g1", "g2", "y0", "y1", "g3", "g4", "z0", "y3", "y2", "y4", "z1", "g5", "zg0", "z3",
    "y5", "zg1", "z2", "z4", "yg0", "zg3", "z5", "yg1", "zg2", "zg4", "c0", "yg3", "zg5", "c1",
    "yg2", "n0", "yg4", "n0", "n0", "n0", "c3", "yg5", "c2", "n0", "n0", "n1", "n1", "n1", "n1",
    "n1", "n1", "c5", "c4",
)


def dot(a, b):
    return jnp.dot(a, b, preferred_element_type=F32)


def dot_t(a, b):
    return lax.dot_general(a, b, (((1,), (1,)), ((), ())), preferred_element_type=F32)


def kernel(
    nh,
    q_hbm, k_hbm, v_hbm, r_hbm, qg_hbm, kg_hbm, w1_hbm, w2_hbm, w3_hbm,
    out,
    q_ref, k_ref, v_ref, r_ref, qg_ref, kg_ref, rb,
    sent, got, wf, wb, t1, t3, hid, d1, d3, kt, ht, e_ref,
    own, cs, cr, ys, yr, zq, zs, zr, zg, x0, xs, xm, x1, u, fw, ob,
    in_sem, a_ss, a_rs, c_ss, c_rs, y_ss, y_rs, z_ss, z_rs,
    zg_ss, zg_rs, yg_ss, yg_rs, cg_ss, cg_rs, o_ss, o_rs,
):
    me_h = lax.axis_index("head")
    me_c = lax.axis_index("ctx")
    y = me_c // (2 * NZ)
    z = (me_c // 2) % NZ
    core = me_c % 2
    tok, width = sent.shape[2], sent.shape[3]
    half = width // 2
    block = half // NY

    def head_peer(s):
        return (me_h + s) % nh

    def ctx_of(yy, zz, cc):
        return (yy * NZ + zz) * 2 + cc

    def z_dev(zz):
        return (me_h, ctx_of(y, zz, core))

    def y_dev(yy):
        return (me_h, ctx_of(yy, z, core))

    core_dev = (me_h, ctx_of(y, z, 1 - core))

    def remote(src, dst, ss, rs, dev):
        return pltpu.make_async_remote_copy(
            src_ref=src, dst_ref=dst, send_sem=ss, recv_sem=rs, device_id=dev, device_id_type=MESH
        )

    barrier = pltpu.get_barrier_semaphore()

    def greet(dev):
        pl.semaphore_signal(barrier, inc=1, device_id=dev, device_id_type=MESH)

    for s in range(1, nh):
        greet((head_peer(s), me_c))
    for s in range(1, NY):
        greet(y_dev((y + s) % NY))
    for s in range(1, NZ):
        greet(z_dev((z + s) % NZ))
    greet(core_dev)

    loads = [
        pltpu.make_async_copy(src, dst, in_sem.at[i])
        for i, (src, dst) in enumerate(
            [
                (k_hbm, k_ref), (kg_hbm, kg_ref), (v_hbm, v_ref), (r_hbm, r_ref),
                (q_hbm, q_ref), (qg_hbm, qg_ref),
                (w1_hbm.at[0], wf.at[0]), (w3_hbm.at[0], wf.at[2]), (w2_hbm.at[0], wf.at[1]),
            ]
        )
    ]
    for copy in loads:
        copy.start()

    def cols(j):
        return pl.ds(pl.multiple_of(j * width, 128), width)

    def send(t, fn):
        def step(s, carry):
            j = head_peer((s + nh // 2 - 2) % (nh - 1) + 1)
            sent[t, j] = fn(j)
            remote(
                sent.at[t, j], got.at[t, me_h], a_ss.at[t, j], a_rs.at[t, me_h], (j, me_c)
            ).start()
            return carry

        lax.fori_loop(1, nh, step, 0)
        got[t, me_h] = fn(me_h)

    def factor_of(x_ref):
        total = jnp.zeros((tok, 1), F32)
        for j in range(nh):
            x = x_ref[:, j * width : (j + 1) * width].astype(F32)
            total = total + jnp.sum(x * x, axis=-1, keepdims=True)
        return lax.rsqrt(total / (nh * width) + epsilon)

    def normalized(x_ref, g_ref, factor):
        return lambda j: (x_ref[:, cols(j)].astype(F32) * factor * g_ref[:, cols(j)]).astype(BF16)

    def arrived(t):
        def step(s, carry):
            j = head_peer(s)
            remote(
                sent.at[t, j], got.at[t, j], a_ss.at[t, j], a_rs.at[t, j], (j, me_c)
            ).wait_recv()
            return carry

        lax.fori_loop(1, nh, step, 0)

    def rated(j):
        wide = jnp.concatenate([rb[j]] * (width // 128), axis=-1)
        return (wide * v_ref[:, cols(j)].astype(F32)).astype(BF16)

    loads[0].wait()
    loads[1].wait()
    factor = factor_of(k_ref)
    pl.semaphore_wait(barrier, nh - 1 + NY - 1 + NZ - 1 + 1)
    send(0, normalized(k_ref, kg_ref, factor))
    loads[2].wait()
    loads[3].wait()
    rate = r_ref[...].astype(F32).T
    for j in range(nh):
        rb[j] = jnp.broadcast_to(rate[:, j : j + 1], (tok, 128))
    send(1, rated)
    loads[4].wait()
    loads[5].wait()
    send(2, normalized(q_ref, qg_ref, factor_of(q_ref)))
    for i in range(3):
        loads[6 + i].wait()
    for i in range(3):
        wb[i] = wf[i].astype(BF16)

    tokens = nh * tok

    def whole(t):
        return got[t].reshape(tokens, width)

    arrived(0)
    p1 = dot(whole(0), wb[0])
    p3 = dot(whole(0), wb[2])
    sig = jax.nn.sigmoid(p1)
    act = p1 * sig
    hid[...] = (act * p3).astype(BF16)
    t3[...] = act
    t1[...] = p3 * sig * (1.0 + p1 * (1.0 - sig))
    kt[...] = whole(0).T
    ht[...] = hid[...].T
    arrived(1)
    e_ref[...] = whole(1)
    back = dot_t(whole(1), wb[1])
    d3[...] = (back * t3[...]).astype(BF16)
    d1[...] = (back * t1[...]).astype(BF16)

    chunks = [(m, slice(a * 128, b * 128)) for m in range(3) for a, b in zip(CUTS, CUTS[1:])]
    per_matrix = len(CUTS) - 1

    def half_rows(cc):
        return pl.ds(pl.multiple_of(cc * half, half), half)

    def core_copy(q):
        m, c = chunks[q]
        return remote(cs.at[m, :, c], cr.at[m, :, c], c_ss.at[q], c_rs.at[q], core_dev)

    def gradient(q, left, right):
        m, c = chunks[q]
        cs[m, :, c] = dot(left[half_rows(1 - core)], right[:, c]).astype(BF16)
        core_copy(q).start()
        own[m, :, c] = dot(left[half_rows(core)], right[:, c])

    def y_rows(j):
        return pl.ds(pl.multiple_of(j * block, 8), block)

    def z_rows(j):
        return pl.ds(pl.multiple_of(j * 16 + (j // 2) * 8, 8), PIECE)

    def y_copy(q, j, src):
        m, c = chunks[q]
        return remote(
            ys.at[m, j, :, c], yr.at[m, src, :, c], y_ss.at[q, j], y_rs.at[q, src], y_dev(j)
        )

    def z_copy(q, j, src):
        m, c = chunks[q]
        return remote(
            zs.at[m, j, :, c], zr.at[m, src, :, c], z_ss.at[q, j], z_rs.at[q, src], z_dev(j)
        )

    def zg_copy(q, j, src):
        m, c = chunks[q]
        slot = zg.at[m, src, :, c]
        return remote(slot, slot, zg_ss.at[q, j], zg_rs.at[q, src], z_dev(j))

    def yg_copy(q, j, src):
        m, c = chunks[q]
        slot = x0.at[m, core, src, :, c]
        return remote(slot, slot, yg_ss.at[q, j], yg_rs.at[q, src], y_dev(j))

    def cg_copy(q, cc, j):
        m, c = chunks[q]
        slot = x0.at[m, cc, j, :, c]
        return remote(slot, slot, cg_ss.at[q, j], cg_rs.at[q, j], core_dev)

    def pair_sum(q, j):
        m, c = chunks[q]
        return own[m, y_rows(j), c] + cr[m, pl.ds(pl.multiple_of(j * block, 16), block), c].astype(F32)

    def start_y(q):
        m, c = chunks[q]
        core_copy(q).wait_recv()
        for s in (2, 1, 3):
            j = (y + s) % NY
            ys[m, j, :, c] = pair_sum(q, j).astype(BF16)
            y_copy(q, j, y).start()

    def start_z(q):
        m, c = chunks[q]
        total = pair_sum(q, y)
        for s in range(1, NY):
            j = (y + s) % NY
            y_copy(q, j, j).wait_recv()
            total = total + yr[m, j, :, c].astype(F32)
        zq[m, :, c] = total
        for s in (2, 1, 3):
            j = (z + s) % NZ
            zs[m, j, :, c] = zq[m, z_rows(j), c].astype(BF16)
            z_copy(q, j, z).start()

    def start_zg(q):
        m, c = chunks[q]
        total = zq[m, z_rows(z), c]
        for s in range(1, NZ):
            j = (z + s) % NZ
            z_copy(q, j, j).wait_recv()
            total = total + zr[m, j, :, c].astype(F32)
        zg[m, z, :, c] = total.astype(BF16)
        for s in (2, 1, 3):
            zg_copy(q, (z + s) % NZ, z).start()

    def start_yg(q):
        m, c = chunks[q]
        for s in range(1, NZ):
            j = (z + s) % NZ
            zg_copy(q, j, j).wait_recv()
        parts = [zg[m, j, :, c].astype(F32) for j in range(NZ)]
        total = jnp.concatenate([parts[0][:16], parts[1], parts[2][:16], parts[3]], axis=0)
        x0[m, core, y, :, c] = total.astype(BF16)
        for s in (2, 1, 3):
            yg_copy(q, (y + s) % NY, y).start()
        cg_copy(q, core, y).start()

    def start_cg(q):
        for s in (1, 3, 2):
            j = (y + s) % NY
            yg_copy(q, j, j).wait_recv()
            cg_copy(q, core, j).start()

    def gathered(m):
        for q in range(per_matrix * m, per_matrix * (m + 1)):
            for j in range(NY):
                cg_copy(q, 1 - core, j).wait_recv()

    def ns_steps(m, w_index):
        cell = {}

        def grad():
            return x0[m].reshape(width, width)

        def square0():
            gathered(m)
            g = grad().astype(F32)
            inv = 1.0 / (jnp.sqrt(jnp.sum(g * g, axis=(0, 1), keepdims=True)) + frob_eps)
            cell["inv"] = inv
            xs[...] = (dot_t(grad(), grad()) * inv * inv).astype(BF16)

        def poly():
            s = xs[...]
            xm[...] = (coeff_b * s.astype(F32) + coeff_c * dot(s, s)).astype(BF16)

        def step0():
            g = grad()
            x1[...] = ((coeff_a * g.astype(F32) + dot(xm[...], g)) * cell["inv"]).astype(BF16)

        def square1():
            xs[...] = dot_t(x1[...], x1[...]).astype(BF16)

        def step1():
            new = (coeff_a * x1[...].astype(F32) + dot(xm[...], x1[...])).astype(BF16)
            u[m] = (wf[w_index] + step_size * new.astype(F32)).astype(BF16)

        return [square0, poly, step0, square1, poly, step1]

    factors = ((kt, d3), (kt, d1), (ht, e_ref))
    iterations = [iter(ns_steps(0, 2)), iter(ns_steps(1, 0))]

    def start_g(q):
        gradient(q, *factors[q // per_matrix])

    stages = {
        "g": start_g, "y": start_y, "z": start_z, "zg": start_zg, "yg": start_yg, "c": start_cg,
    }
    for event in ORDER:
        name, index = event[:-1], int(event[-1])
        if name == "n":
            next(iterations[index])()
        else:
            stages[name](index)

    arrived(2)
    a = dot(whole(2), u[1])
    b = dot(whole(2), u[0])
    fw[...] = (a * jax.nn.sigmoid(a) * b).astype(BF16)
    for fn in ns_steps(2, 1):
        fn()

    def o_copy(j, src):
        return remote(ob.at[j], out.at[src], o_ss.at[j], o_rs.at[src], (j, me_c))

    chunk = 2 * tok
    n_chunks = tokens // chunk
    mine = me_h // 2

    def finish(i):
        c = (mine + i) % n_chunks
        rows = pl.ds(pl.multiple_of(c * chunk, chunk), chunk)
        o = dot(fw[rows], u[2])
        o = o * lax.rsqrt(jnp.mean(o * o, axis=-1, keepdims=True) + epsilon)
        ob[pl.ds(2 * c, 2)] = o.astype(BF16).reshape(2, tok, width)
        return c

    def others(i, carry):
        c = finish(i)
        o_copy(2 * c, me_h).start()
        o_copy(2 * c + 1, me_h).start()
        return carry

    lax.fori_loop(1, n_chunks, others, 0)
    finish(0)
    o_copy(mine * 2 + (1 - me_h % 2), me_h).start()
    keep = pltpu.make_async_copy(ob.at[me_h], out.at[me_h], in_sem.at[0])
    keep.start()

    for q in range(len(chunks)):
        core_copy(q).wait_send()
        for s in range(1, NY):
            y_copy(q, (y + s) % NY, y).wait_send()
            yg_copy(q, (y + s) % NY, y).wait_send()
        for s in range(1, NZ):
            z_copy(q, (z + s) % NZ, z).wait_send()
            zg_copy(q, (z + s) % NZ, z).wait_send()
        for j in range(NY):
            cg_copy(q, core, j).wait_send()

    def returned(s, carry):
        j = head_peer(s)
        for t in range(3):
            remote(
                sent.at[t, j], got.at[t, j], a_ss.at[t, j], a_rs.at[t, j], (j, me_c)
            ).wait_send()
        o_copy(j, me_h).wait_send()
        o_copy(j, j).wait_recv()
        return carry

    lax.fori_loop(1, nh, returned, 0)
    keep.wait()


def per_device(queries, keys, values, rates, q_gain, k_gain, w_first, w_second, w_third):
    nh = rates.shape[1]
    tok, model = queries.shape
    width = model // nh
    tokens = nh * tok
    half = width // 2
    block = half // NY
    hbm = pl.BlockSpec(memory_space=pl.ANY)

    def dma(*shape):
        return pltpu.SemaphoreType.DMA(shape)

    out = pl.pallas_call(
        functools.partial(kernel, nh),
        out_shape=jax.ShapeDtypeStruct((nh, tok, width), BF16),
        in_specs=[hbm] * 9,
        out_specs=hbm,
        scratch_shapes=[
            pltpu.VMEM((tok, model), BF16),
            pltpu.VMEM((tok, model), BF16),
            pltpu.VMEM((tok, model), BF16),
            pltpu.VMEM((nh, tok), BF16),
            pltpu.VMEM((1, model), F32),
            pltpu.VMEM((1, model), F32),
            pltpu.VMEM((nh, tok, 128), F32),
            pltpu.VMEM((3, nh, tok, width), BF16),
            pltpu.VMEM((3, nh, tok, width), BF16),
            pltpu.VMEM((3, width, width), F32),
            pltpu.VMEM((3, width, width), BF16),
            pltpu.VMEM((tokens, width), F32),
            pltpu.VMEM((tokens, width), F32),
            pltpu.VMEM((tokens, width), BF16),
            pltpu.VMEM((tokens, width), BF16),
            pltpu.VMEM((tokens, width), BF16),
            pltpu.VMEM((width, tokens), BF16),
            pltpu.VMEM((width, tokens), BF16),
            pltpu.VMEM((tokens, width), BF16),
            pltpu.VMEM((3, half, width), F32),
            pltpu.VMEM((3, half, width), BF16),
            pltpu.VMEM((3, half, width), BF16),
            *[pltpu.VMEM((3, NY, block, width), BF16)] * 2,
            pltpu.VMEM((3, block, width), F32),
            pltpu.VMEM((3, NZ, PIECE, width), BF16),
            pltpu.VMEM((3, NZ, PIECE, width), BF16),
            pltpu.VMEM((3, NZ, PIECE, width), BF16),
            pltpu.VMEM((3, 2, NY, block, width), BF16),
            pltpu.VMEM((width, width), BF16),
            pltpu.VMEM((width, width), BF16),
            pltpu.VMEM((width, width), BF16),
            pltpu.VMEM((3, width, width), BF16),
            pltpu.VMEM((tokens, width), BF16),
            pltpu.VMEM((nh, tok, width), BF16),
            dma(9),
            dma(3, nh), dma(3, nh),
            dma(6), dma(6),
            *[dma(6, NY)] * 2,
            *[dma(6, NZ)] * 4,
            *[dma(6, NY)] * 4,
            dma(nh), dma(nh),
        ],
        compiler_params=pltpu.CompilerParams(
            collective_id=0, has_side_effects=True, vmem_limit_bytes=VMEM_LIMIT
        ),
        name="span",
    )(
        queries, keys, values, rates.T, q_gain.reshape(1, model), k_gain.reshape(1, model),
        w_first, w_second, w_third,
    )
    return out.transpose(1, 0, 2).reshape(tok, model)


def solution(mesh):
    return jax.shard_map(
        per_device,
        mesh=mesh,
        in_specs=(
            P(("head", "ctx"), None),
            P(("head", "ctx"), None),
            P(("head", "ctx"), None),
            P(("head", "ctx"), None),
            P(),
            P(),
            P("head", None, None),
            P("head", None, None),
            P("head", None, None),
        ),
        out_specs=P(("head", "ctx"), None),
        check_vma=False,
    )
```
